32 devices in a mesh: row: 4 (over z), col: 8 (over y, x, core).
Axes of the slice: x: 2, y: 2, z: 4, core: 2. Of those that a mesh axis runs over, the one named last changes fastest.
Arguments:
- grad_first: float32 [4096, 20480], P('row', 'col'), may hold values from -1000 to 1000
- grad_second: float32 [4096, 20480], P('row', 'col'), may hold values from -1000 to 1000
Outputs:
- update: float32 [4096, 20480], P('row', 'col')
The draws below stay inside these ranges and needn't reach their ends.
All inputs are finite; a program needn't handle non-finite values.
Results may differ from the reference program's by a relative error of at most 0.00014.
Values sent between devices are 32-bit elements; how exact they have to be, the bound alone decides.
A program may use at most 128 MiB of HBM per device.

```python
import math
import jax
import jax.numpy as jnp
from jax import lax

D = 4096
FF = 20480
BLOCK = 256
ITERS = 6


def gradient_draw(key, step_number):
    own_key = jax.random.fold_in(key, 101 + step_number)
    row_key = jax.random.fold_in(key, 211)
    col_key = jax.random.fold_in(key, 223)
    upper_scale = 3.0
    entries = jax.random.normal(own_key, (D, FF), jnp.float32)
    row_scale = jnp.exp(jax.random.uniform(row_key, (D,), jnp.float32, 0.0, math.log(upper_scale)))
    col_scale = jnp.exp(jax.random.uniform(col_key, (FF,), jnp.float32, 0.0, math.log(upper_scale)))
    return entries * row_scale[:, None] * col_scale[None, :]


def draw_grad_first(key, part):
    return gradient_draw(key, 0)


def draw_grad_second(key, part):
    return gradient_draw(key, 1)


def setup_inputs(seed: int = 0) -> dict:
    streams_of = jax.random.split(jax.random.key(seed), 3)
    grad_first = draw_grad_first(jax.random.fold_in(streams_of[2], 71), 0)
    grad_second = draw_grad_second(jax.random.fold_in(streams_of[2], 71), 0)
    return dict(grad_first=grad_first, grad_second=grad_second)


damping = 0.001

def batched(left_mat, right_mat):
    return jnp.einsum('kij,kjl->kil', left_mat, right_mat, precision=lax.Precision.HIGHEST)

def newton_roots(statistic):
    width = statistic.shape[-1]
    identity = jnp.eye(width, dtype=jnp.float32)
    damped = statistic + damping * identity
    frob_norm = jnp.sqrt(lax.optimization_barrier(jnp.sum(damped * damped, axis=(1, 2))))
    scaled = damped / frob_norm[:, None, None]
    current = identity[None] * lax.rsqrt(jnp.sqrt(frob_norm))[:, None, None]
    for iteration in range(ITERS):
        factor = (5.0 * identity - scaled) / 4.0
        current = batched(current, factor)
        square = batched(factor, factor)
        scaled = batched(batched(square, square), scaled)
    return current

def reference(grad_first, grad_second):
    left_count = D // BLOCK
    right_count = FF // BLOCK
    left_state = jnp.zeros((left_count, BLOCK, BLOCK), jnp.float32)
    right_state = jnp.zeros((right_count, BLOCK, BLOCK), jnp.float32)
    update = jnp.zeros((D, FF), jnp.float32)
    for gradient in (grad_first, grad_second):
        row_blocks = gradient.reshape(left_count, BLOCK, FF)
        col_blocks = gradient.reshape(D, right_count, BLOCK)
        left_state = left_state + jnp.einsum('bik,bjk->bij', row_blocks, row_blocks, precision=lax.Precision.HIGHEST) / FF
        right_state = right_state + jnp.einsum('kbi,kbj->bij', col_blocks, col_blocks, precision=lax.Precision.HIGHEST) / D
        left_factor = newton_roots(left_state)
        right_factor = newton_roots(right_state)
        halfway = jnp.einsum('bij,bjk->bik', left_factor, row_blocks, precision=lax.Precision.HIGHEST).reshape(D, right_count, BLOCK)
        update = update + jnp.einsum('kbi,bij->kbj', halfway, right_factor, precision=lax.Precision.HIGHEST).reshape(D, FF)
    return update
```

```python
import functools

import jax
import jax.numpy as jnp
from jax import lax
from jax.experimental import pallas as pl
from jax.experimental.pallas import tpu as pltpu
from jax.sharding import PartitionSpec as P

BLOCK = 256
HALF = 128
PACKED = BLOCK + 8
ITERS = 6
damping = 0.001
VMEM_LIMIT = 56 * 1024 * 1024


def split(value):
    high = value.astype(jnp.bfloat16)
    low = (value - high.astype(jnp.float32)).astype(jnp.bfloat16)
    return high, low


def dot(left, right, dims=(((1,), (0,)), ((), ()))):
    return lax.dot_general(left, right, dims, preferred_element_type=jnp.float32)


def product(left, right):
    return dot(
        jnp.concatenate([left[0], left[0], left[1]], axis=1),
        jnp.concatenate([right[0], right[1], right[0]], axis=0),
    )


def indices():
    rows = lax.broadcasted_iota(jnp.int32, (HALF, HALF), 0)
    cols = lax.broadcasted_iota(jnp.int32, (HALF, HALF), 1)
    return rows, cols


def pack(write, block):
    rows, cols = indices()
    first, last = block[:HALF, :HALF], block[HALF:, HALF:]
    write(0, HALF, block[:HALF, HALF:])
    write(HALF, HALF, jnp.where(rows <= cols, first, last))
    diagonal = jnp.sum(jnp.where(rows == cols, last, 0.0), axis=0, keepdims=True)
    write(BLOCK, 8, jnp.broadcast_to(diagonal, (8, HALF)))


def unpack(packed):
    rows, cols = indices()
    off = packed[:HALF]
    tile = packed[HALF:BLOCK]
    turned = tile.T
    first = jnp.where(rows <= cols, tile, turned)
    last = jnp.where(rows > cols, tile, jnp.where(rows < cols, turned, packed[BLOCK : BLOCK + 1]))
    return jnp.concatenate(
        [jnp.concatenate([first, off], axis=1), jnp.concatenate([off.T, last], axis=1)], axis=0
    )


def writer(ref, *lead):
    def write(start, size, value):
        ref[(*lead, pl.ds(start, size), slice(None))] = value

    return write


def left_stat_kernel(g1_ref, g2_ref, out_ref):
    total = None
    for step, ref in enumerate((g1_ref, g2_ref)):
        high, low = split(ref[...])
        both = dot(high, jnp.concatenate([high, low], axis=0), (((1,), (1,)), ((), ())))
        cross = both[:, BLOCK:]
        part = both[:, :BLOCK] + (cross + cross.T)
        total = part if total is None else total + part
        pack(writer(out_ref, step, 0), total)


def right_stat_kernel(g1_ref, g2_ref, out_ref):
    total = None
    for step, ref in enumerate((g1_ref, g2_ref)):
        high, low = split(ref[...])
        both = dot(high.T, jnp.concatenate([high, low], axis=1))
        cross = both[:, BLOCK:]
        part = both[:, :BLOCK] + (cross + cross.T)
        total = part if total is None else total + part
        pack(writer(out_ref, step, 0), total)


def stats(kernel, grads, count, tile, index):
    flops = 8 * grads[0].size * BLOCK
    return pl.pallas_call(
        kernel,
        grid=(count,),
        in_specs=[pl.BlockSpec(tile, index)] * 2,
        out_specs=pl.BlockSpec((2, 1, PACKED, HALF), lambda i: (0, i, 0, 0)),
        out_shape=jax.ShapeDtypeStruct((2, count, PACKED, HALF), jnp.float32),
        compiler_params=pltpu.CompilerParams(vmem_limit_bytes=VMEM_LIMIT),
        cost_estimate=pl.CostEstimate(
            flops=flops, bytes_accessed=8 * grads[0].size, transcendentals=0
        ),
    )(*grads)


def root_kernel(count, scale, stat_ref, out_ref, x_ref, m_ref):
    rows = lax.broadcasted_iota(jnp.int32, (BLOCK, BLOCK), 0)
    cols = lax.broadcasted_iota(jnp.int32, (BLOCK, BLOCK), 1)
    identity = jnp.where(rows == cols, 1.0, 0.0)

    def factor_of(scaled):
        return (5.0 * identity - scaled) / 4.0

    def advance(factor_parts, scaled):
        square = product(factor_parts, factor_parts)
        square_parts = split(square)
        fourth = product(square_parts, square_parts)
        return product(split(fourth), split(scaled))

    for slot in range(count):
        damped = unpack(stat_ref[slot]) * scale + damping * identity
        total = jnp.sum(jnp.sum(damped * damped, axis=0, keepdims=True), axis=1, keepdims=True)
        norm = jnp.sqrt(total)
        scaled = damped / norm
        factor = factor_of(scaled)
        x_ref[slot] = factor * lax.rsqrt(jnp.sqrt(norm))
        m_ref[slot] = advance(split(factor), scaled)

    def step(iteration, carry):
        for slot in range(count):
            scaled = m_ref[slot]
            parts = split(factor_of(scaled))
            x_ref[slot] = product(split(x_ref[slot]), parts)
            m_ref[slot] = advance(parts, scaled)
        return carry

    lax.fori_loop(0, ITERS - 2, step, 0)
    for slot in range(count):
        result = product(split(x_ref[slot]), split(factor_of(m_ref[slot])))
        pack(writer(out_ref, slot), result)


def roots(statistic, scale):
    count = statistic.shape[0]
    return pl.pallas_call(
        functools.partial(root_kernel, count, scale),
        out_shape=jax.ShapeDtypeStruct(statistic.shape, jnp.float32),
        scratch_shapes=[pltpu.VMEM((count, BLOCK, BLOCK), jnp.float32)] * 2,
        compiler_params=pltpu.CompilerParams(vmem_limit_bytes=VMEM_LIMIT),
        cost_estimate=pl.CostEstimate(
            flops=count * 20 * 6 * BLOCK**3, bytes_accessed=2 * statistic.size * 4, transcendentals=0
        ),
    )(statistic)


def left_apply_kernel(g1_ref, g2_ref, l1_ref, l2_ref, high_ref, low_ref):
    for step, (g_ref, l_ref) in enumerate(((g1_ref, l1_ref), (g2_ref, l2_ref))):
        half = product(split(unpack(l_ref[0])), split(g_ref[...]))
        high, low = split(half)
        high_ref[step] = high
        low_ref[step] = low


def left_apply(grads, packed, count):
    rows, cols = grads[0].shape
    tiles = 2 if cols % (2 * HALF) == 0 else 1
    width = cols // tiles
    root_spec = lambda first: pl.BlockSpec((1, PACKED, HALF), lambda b, t: (first + b, 0, 0))
    out_spec = pl.BlockSpec((2, BLOCK, width), lambda b, t: (0, b, t))
    return pl.pallas_call(
        left_apply_kernel,
        grid=(count, tiles),
        in_specs=[pl.BlockSpec((BLOCK, width), lambda b, t: (b, t))] * 2
        + [root_spec(0), root_spec(count)],
        out_specs=[out_spec] * 2,
        out_shape=[jax.ShapeDtypeStruct((2, rows, cols), jnp.bfloat16)] * 2,
        compiler_params=pltpu.CompilerParams(vmem_limit_bytes=VMEM_LIMIT),
        cost_estimate=pl.CostEstimate(
            flops=12 * rows * cols * BLOCK, bytes_accessed=16 * rows * cols, transcendentals=0
        ),
    )(*grads, packed, packed)


def right_apply_kernel(high_ref, low_ref, r1_ref, r2_ref, out_ref):
    lefts, rights = [], []
    for step, r_ref in enumerate((r1_ref, r2_ref)):
        high, low = split(unpack(r_ref[0]))
        lefts += [high_ref[step], high_ref[step], low_ref[step]]
        rights += [high, low, high]
    out_ref[...] = dot(jnp.concatenate(lefts, axis=1), jnp.concatenate(rights, axis=0))


def right_apply(high, low, packed, count):
    _, rows, cols = high.shape
    root_spec = lambda first: pl.BlockSpec((1, PACKED, HALF), lambda j: (first + j, 0, 0))
    half_spec = pl.BlockSpec((2, rows, BLOCK), lambda j: (0, 0, j))
    return pl.pallas_call(
        right_apply_kernel,
        grid=(count,),
        in_specs=[half_spec, half_spec, root_spec(0), root_spec(count)],
        out_specs=pl.BlockSpec((rows, BLOCK), lambda j: (0, j)),
        out_shape=jax.ShapeDtypeStruct((rows, cols), jnp.float32),
        compiler_params=pltpu.CompilerParams(vmem_limit_bytes=VMEM_LIMIT),
        cost_estimate=pl.CostEstimate(
            flops=12 * rows * cols * BLOCK, bytes_accessed=12 * rows * cols, transcendentals=0
        ),
    )(high, low, packed, packed)


def scatter(packed, axis):
    devices = lax.axis_size(axis)
    flat = packed.reshape(-1, PACKED, HALF)
    extra = -flat.shape[0] % devices
    if extra:
        flat = jnp.concatenate([flat, jnp.zeros((extra, PACKED, HALF), jnp.float32)], axis=0)
    return lax.psum_scatter(flat, axis, scatter_dimension=0, tiled=True)


def body(grad_first, grad_second):
    grads = (grad_first, grad_second)
    rows, cols = grad_first.shape
    left_count, right_count = rows // BLOCK, cols // BLOCK
    left_scale = 1.0 / (cols * lax.axis_size("col"))
    right_scale = 1.0 / (rows * lax.axis_size("row"))
    left_part = stats(left_stat_kernel, grads, left_count, (BLOCK, cols), lambda i: (i, 0))
    right_part = stats(right_stat_kernel, grads, right_count, (rows, BLOCK), lambda i: (0, i))
    left_sum = scatter(left_part, "col")
    right_sum = scatter(right_part, "row")
    left_roots = lax.all_gather(roots(left_sum, left_scale), "col", axis=0, tiled=True)
    right_own = roots(right_sum, right_scale)
    right_roots = lax.all_gather(right_own, "row", axis=0, tiled=True)
    high, low = left_apply(grads, left_roots, left_count)
    return right_apply(high, low, right_roots, right_count)


def solution(mesh):
    in_specs = (P("row", "col"), P("row", "col"))
    out_specs = P("row", "col")
    return jax.shard_map(body, mesh=mesh, in_specs=in_specs, out_specs=out_specs, check_vma=False)
```
